32 devices in a mesh: tm: 4 (over x, core), freq: 8 (over z, y).
Axes of the slice: x: 2, y: 2, z: 4, core: 2. Of those that a mesh axis runs over, the one named last changes fastest.
Arguments:
- visibilities: float32 [2, 4, 32, 8, 2016], P(None, None, 'tm', 'freq'), may hold values from -48 to 48
- sky_model: float32 [2, 4, 32, 8, 2016], P(None, None, 'tm', 'freq'), may hold values from -3 to 3
- gain_time: float32 [2, 2, 8, 64], P(None, None, 'tm'), may hold values from -4 to 4
- gain_band: float32 [2, 2, 8, 64], P(None, None, 'freq'), may hold values from -2.5 to 2.5
- delay_start: float32 [2, 64], replicated, may hold values from -2.2 to 2.2
- first_antenna: int32 [2016], replicated, may hold values from 0 to 63, as said below
- second_antenna: int32 [2016], replicated, may hold values from 0 to 63
Outputs:
- solved_time: float32 [2, 2, 8, 64], P(None, None, 'tm')
- solved_band: float32 [2, 2, 8, 64], P(None, None, 'freq')
- solved_delay: float32 [2, 64], replicated
- weights: float32 [32, 2016], P('tm')
- residual: float32 [2, 4, 32, 8, 2016], P(None, None, 'tm', 'freq')
The draws below stay inside these ranges and needn't reach their ends.
Inputs may be any that keep to these rules, and one draw needn't show every extreme that they name: first_antenna and second_antenna together name every unordered pair of distinct antennas of the 64 exactly once, in an order and orientation drawn from the seed.
All inputs are finite; a program needn't handle non-finite values.
Results may differ from the reference program's by a relative error of at most 0.00013.
Values sent between devices are 32-bit elements; how exact they have to be, the bound alone decides.
A program may use at most 64 MiB of HBM per device.

```python
import math
import jax
import jax.numpy as jnp
import numpy as np
from jax import lax

ANTENNA_COUNT = 64
BL = 2016
INTERVAL_TIMES = 4
SWEEPS = 2
TIMES = 32
CHANNEL_COUNT = 8
INTERVAL_COUNT = 8


def clipped_values(key, dims):
    return jax.random.truncated_normal(key, -3.0, 3.0, dims, jnp.float32)


def polar_complex(amplitude, angles):
    return jnp.stack([amplitude * jnp.cos(angles), amplitude * jnp.sin(angles)])


def product_drawn(former, latter):
    return jnp.stack([former[0] * latter[0] - former[1] * latter[1], former[0] * latter[1] + former[1] * latter[0]])


def observation(key):
    split_keys = [jax.random.fold_in(key, 7100 + number) for number in range(16)]
    smaller_antenna, larger_antenna = np.triu_indices(ANTENNA_COUNT, 1)
    ordering = jax.random.permutation(split_keys[0], BL)
    swapped = jax.random.randint(split_keys[1], (BL,), 0, 2)
    lesser_ids = jnp.asarray(smaller_antenna, jnp.int32)[ordering]
    greater_ids = jnp.asarray(larger_antenna, jnp.int32)[ordering]
    first_antenna = jnp.where(swapped == 1, greater_ids, lesser_ids)
    second_antenna = jnp.where(swapped == 1, lesser_ids, greater_ids)
    time_magnitude = jnp.exp(0.2 * clipped_values(split_keys[2], (2, INTERVAL_COUNT, ANTENNA_COUNT)))
    time_phases = jax.random.uniform(split_keys[3], (2, INTERVAL_COUNT, ANTENNA_COUNT), jnp.float32, -math.pi, math.pi)
    bandpass_magnitude = jnp.exp(0.15 * clipped_values(split_keys[4], (2, CHANNEL_COUNT, ANTENNA_COUNT)))
    bandpass_phases = 0.6 * clipped_values(split_keys[5], (2, CHANNEL_COUNT, ANTENNA_COUNT))
    actual_delay = jax.random.uniform(split_keys[6], (2, ANTENNA_COUNT), jnp.float32, -2.0, 2.0)
    initial_time_gain = polar_complex(time_magnitude * jnp.exp(0.25 * clipped_values(split_keys[7], (2, INTERVAL_COUNT, ANTENNA_COUNT))), time_phases + 0.3 * clipped_values(split_keys[8], (2, INTERVAL_COUNT, ANTENNA_COUNT)))
    initial_bandpass = polar_complex(bandpass_magnitude * jnp.exp(0.15 * clipped_values(split_keys[9], (2, CHANNEL_COUNT, ANTENNA_COUNT))), bandpass_phases + 0.3 * clipped_values(split_keys[10], (2, CHANNEL_COUNT, ANTENNA_COUNT)))
    initial_delay = actual_delay + jax.random.uniform(split_keys[11], (2, ANTENNA_COUNT), jnp.float32, -0.15, 0.15)
    frequency = (jnp.arange(CHANNEL_COUNT, dtype=jnp.float32) + 0.5) / CHANNEL_COUNT - 0.5
    amplitude = jnp.repeat(time_magnitude, INTERVAL_TIMES, axis=1)[:, :, None, :] * bandpass_magnitude[:, None]
    angles = jnp.repeat(time_phases, INTERVAL_TIMES, axis=1)[:, :, None, :] + bandpass_phases[:, None] + 2.0 * math.pi * actual_delay[:, None, None, :] * frequency[None, None, :, None]
    left_amplitude = amplitude[..., first_antenna]
    right_amplitude = amplitude[..., second_antenna]
    left_angles = angles[..., first_antenna]
    right_angles = angles[..., second_antenna]
    corruption = polar_complex(left_amplitude[:, None] * right_amplitude[None], left_angles[:, None] - right_angles[None])
    cells = (2, 2, 2, TIMES, CHANNEL_COUNT, BL)
    sky_cells = clipped_values(split_keys[12], cells)
    noise = clipped_values(split_keys[13], cells)
    by_baseline = jnp.exp(jax.random.uniform(split_keys[14], (BL,), jnp.float32, 0.0, math.log(10.0)))
    by_time = jnp.exp(jax.random.uniform(split_keys[15], (TIMES,), jnp.float32, 0.0, math.log(3.0)))
    by_channel = 1.0 + 2.0 * jnp.arange(CHANNEL_COUNT, dtype=jnp.float32) / (CHANNEL_COUNT - 1)
    level = 0.02 * by_time[:, None, None] * by_channel[None, :, None] * by_baseline[None, None, :]
    observed = product_drawn(corruption, sky_cells) + noise * level
    return {'visibilities': observed.reshape(2, 4, TIMES, CHANNEL_COUNT, BL), 'sky_model': sky_cells.reshape(2, 4, TIMES, CHANNEL_COUNT, BL), 'gain_time': initial_time_gain, 'gain_band': initial_bandpass, 'delay_start': initial_delay, 'antenna_one': first_antenna, 'antenna_two': second_antenna}


def draw_visibilities(key, part):
    return observation(key)['visibilities']


def draw_sky_model(key, part):
    return observation(key)['sky_model']


def draw_gain_time(key, part):
    return observation(key)['gain_time']


def draw_gain_band(key, part):
    return observation(key)['gain_band']


def draw_delay_start(key, part):
    return observation(key)['delay_start']


def draw_first_antenna(key, part):
    return observation(key)['antenna_one']


def draw_second_antenna(key, part):
    return observation(key)['antenna_two']


def setup_inputs(seed: int = 0) -> dict:
    keys = jax.random.split(jax.random.key(seed), 8)
    visibilities = draw_visibilities(jax.random.fold_in(keys[7], 71), 0)
    sky_model = draw_sky_model(jax.random.fold_in(keys[7], 71), 0)
    gain_time = draw_gain_time(jax.random.fold_in(keys[7], 71), 0)
    gain_band = draw_gain_band(jax.random.fold_in(keys[7], 71), 0)
    delay_start = draw_delay_start(jax.random.fold_in(keys[7], 71), 0)
    first_antenna = draw_first_antenna(jax.random.fold_in(keys[7], 71), 0)
    second_antenna = draw_second_antenna(jax.random.fold_in(keys[7], 71), 0)
    return dict(visibilities=visibilities, sky_model=sky_model, gain_time=gain_time, gain_band=gain_band, delay_start=delay_start, first_antenna=first_antenna, second_antenna=second_antenna)


FULL_TURN = 2.0 * math.pi
DAMPING = 0.5
EPSILON = 1e-6
PRECISE = lax.Precision.HIGHEST


def product(former, latter):
    return jnp.stack([former[0] * latter[0] - former[1] * latter[1], former[0] * latter[1] + former[1] * latter[0]])


def conjugate(value_array):
    return jnp.stack([value_array[0], -value_array[1]])


def magnitude(value_array):
    return value_array[0] * value_array[0] + value_array[1] * value_array[1]


def selector_mask(antennas, number):
    return (antennas[:, None] == jnp.arange(number, dtype=jnp.int32)[None, :]).astype(jnp.float32)


def to_antennas(value_array, gather_table):
    leading = value_array.shape[:-1]
    flattened = value_array.reshape(-1, value_array.shape[-1])
    summed = jnp.dot(flattened, gather_table, precision=PRECISE, preferred_element_type=jnp.float32)
    return summed.reshape(leading + (gather_table.shape[1],))


def chain_gains(gain_row_stack, bandpass, delays, frequency):
    angles = FULL_TURN * delays[:, None, :] * frequency[None, :, None]
    phasor = jnp.stack([jnp.cos(angles), jnp.sin(angles)])
    band_delay = product(bandpass, phasor)
    combined_gain = product(gain_row_stack[:, :, :, None], band_delay[:, :, None])
    return combined_gain, band_delay, phasor


def evaluate(visibilities, sky_model, gain_row_stack, bandpass, delays, frequency, first_antenna, second_antenna, first_gather, second_gather, weights, purpose):
    combined_gain, band_delay, phasor = chain_gains(gain_row_stack, bandpass, delays, frequency)
    cells = (2, 2, 2) + visibilities.shape[2:]
    observed = visibilities.reshape(cells)
    sky_cells = sky_model.reshape(cells)
    left_side_gain = jnp.take(combined_gain, first_antenna, axis=-1)[:, :, None]
    right_side_gain = jnp.take(combined_gain, second_antenna, axis=-1)[:, None]
    partial_value = product(left_side_gain, sky_cells)
    predicted = product(partial_value, conjugate(right_side_gain))
    residual = observed - predicted
    if purpose == "residual":
        return residual.reshape(visibilities.shape)
    if purpose == "noise":
        return magnitude(residual).sum(axis=(0, 1, 3))
    weighted = weights[:, None, :]
    if purpose == "delay":
        turning = FULL_TURN * frequency[:, None]
        crossed = predicted[0] * residual[1] - predicted[1] * residual[0]
        numerator_terms = weighted * turning * crossed
        denominator_terms = weighted * turning * turning * magnitude(predicted)
        numerator = to_antennas(numerator_terms.sum(axis=1), first_gather) - to_antennas(numerator_terms.sum(axis=0), second_gather)
        denominator = to_antennas(denominator_terms.sum(axis=1), first_gather) + to_antennas(denominator_terms.sum(axis=0), second_gather)
        return numerator, denominator
    if purpose == "time":
        remaining_terms = jnp.broadcast_to(band_delay[:, :, None], combined_gain.shape)
    else:
        remaining_terms = product(gain_row_stack[:, :, :, None], phasor[:, :, None])
    remaining_left = jnp.take(remaining_terms, first_antenna, axis=-1)[:, :, None]
    remaining_right = jnp.take(remaining_terms, second_antenna, axis=-1)[:, None]
    forward = product(remaining_left, product(sky_cells, conjugate(right_side_gain)))
    backward = product(conjugate(partial_value), remaining_right)
    lead_terms = weighted * product(conjugate(forward), residual)
    trail_terms = weighted * conjugate(product(backward, residual))
    lead_power = weighted * magnitude(forward)
    trail_power = weighted * magnitude(backward)
    numerator = to_antennas(lead_terms.sum(axis=2), first_gather) + to_antennas(trail_terms.sum(axis=1), second_gather)
    denominator = to_antennas(lead_power.sum(axis=1), first_gather) + to_antennas(trail_power.sum(axis=0), second_gather)
    return numerator, denominator


def reference(visibilities, sky_model, gain_time, gain_band, delay_start, first_antenna, second_antenna):
    first_gather = selector_mask(first_antenna, ANTENNA_COUNT)
    second_gather = selector_mask(second_antenna, ANTENNA_COUNT)
    frequency = (jnp.arange(CHANNEL_COUNT, dtype=jnp.int32).astype(jnp.float32) + 0.5) / CHANNEL_COUNT - 0.5

    def sweep_data(purpose, solved_time, solved_band, solved_delay, weights):
        def per_interval(interval):
            observed = lax.dynamic_slice_in_dim(visibilities, interval * INTERVAL_TIMES, INTERVAL_TIMES, 2)
            sky_cells = lax.dynamic_slice_in_dim(sky_model, interval * INTERVAL_TIMES, INTERVAL_TIMES, 2)
            column_index = lax.dynamic_slice_in_dim(solved_time, interval, 1, 2)
            gain_row_stack = jnp.broadcast_to(column_index, (2, 2, INTERVAL_TIMES, ANTENNA_COUNT))
            weight_rows = lax.dynamic_slice_in_dim(weights, interval * INTERVAL_TIMES, INTERVAL_TIMES, 0)
            result = evaluate(observed, sky_cells, gain_row_stack, solved_band, solved_delay, frequency, first_antenna, second_antenna, first_gather, second_gather, weight_rows, purpose)
            if purpose == "time":
                return result[0].sum(axis=(2, 3)), result[1].sum(axis=(1, 2))
            if purpose == "band":
                return result[0].sum(axis=2), result[1].sum(axis=1)
            if purpose == "delay":
                return result[0].sum(axis=(1, 2)), result[1].sum(axis=(1, 2))
            return result

        return lax.map(per_interval, jnp.arange(INTERVAL_COUNT, dtype=jnp.int32))

    solved_time, solved_band, solved_delay = gain_time, gain_band, delay_start
    weights = jnp.ones((TIMES, BL), jnp.float32)
    for repeat in range(SWEEPS):
        noise_power = sweep_data("noise", solved_time, solved_band, solved_delay, weights).reshape(TIMES, BL)
        weights = 1.0 / (noise_power / (4 * CHANNEL_COUNT) + EPSILON)
        numerator, denominator = sweep_data("time", solved_time, solved_band, solved_delay, weights)
        numerator = jnp.moveaxis(numerator, 0, 2)
        denominator = jnp.moveaxis(denominator, 0, 1)
        solved_time = solved_time + DAMPING * numerator / denominator
        numerator, denominator = sweep_data("band", solved_time, solved_band, solved_delay, weights)
        solved_band = solved_band + DAMPING * numerator.sum(axis=0) / denominator.sum(axis=0)
        numerator, denominator = sweep_data("delay", solved_time, solved_band, solved_delay, weights)
        solved_delay = solved_delay + DAMPING * numerator.sum(axis=0) / denominator.sum(axis=0)
    blocks = sweep_data("residual", solved_time, solved_band, solved_delay, weights)
    residual = jnp.moveaxis(blocks, 0, 2).reshape(2, 4, TIMES, CHANNEL_COUNT, BL)
    return solved_time, solved_band, solved_delay, weights, residual
```

```python
import functools
import math

import jax
import jax.numpy as jnp
from jax import lax
from jax.experimental import pallas as pl
from jax.experimental.pallas import tpu as pltpu
from jax.sharding import PartitionSpec as P

INTERVAL_TIMES = 4
SWEEPS = 2
FULL_TURN = 2.0 * math.pi
DAMPING = 0.5
EPSILON = 1e-06
LANES = 128
POLS = 2
UNROLLED_PEERS = 8


def cmul(a, b):
    return (a[0] * b[0] - a[1] * b[1], a[0] * b[1] + a[1] * b[0])


def conj_mul(a, b):
    return (a[0] * b[0] + a[1] * b[1], a[0] * b[1] - a[1] * b[0])


def power(a):
    return a[0] * a[0] + a[1] * a[1]


def split3(x):
    high = x.astype(jnp.bfloat16)
    rest = x - high.astype(jnp.float32)
    middle = rest.astype(jnp.bfloat16)
    low = (rest - middle.astype(jnp.float32)).astype(jnp.bfloat16)
    return high, middle, low


def each_peer(count, action):
    if count <= UNROLLED_PEERS:
        for step in range(1, count):
            action(step)
    else:
        lax.fori_loop(1, count, lambda step, carry: (action(step), carry)[1], 0)


def maybe(condition, action):
    if condition is True:
        action()
    else:
        pl.when(condition)(action)


def kernel(
    sizes,
    vis,
    sky,
    params,
    first,
    second,
    out_params,
    out_weights,
    out_residual,
    hot,
    u_ref,
    q_ref,
    wide,
    terms,
    s_ref,
    rs_ref,
    w_ref,
    time_ref,
    band_ref,
    turn_tm_ref,
    turn_ref,
    rs_sem,
    ag_sem,
    time_sem,
    band_sem,
    turn_tm_sem,
    turn_sem,
):
    n_freq, n_tm, channels, times, baselines, chunks, width = sizes
    intervals = times // INTERVAL_TIMES
    ants = LANES // POLS
    padded = chunks * width
    f_me = lax.axis_index("freq")
    t_me = lax.axis_index("tm")

    barrier = pltpu.get_barrier_semaphore()

    def greet(axis, count, me):
        def one(step):
            pl.semaphore_signal(
                barrier,
                inc=1,
                device_id={axis: lax.rem(me + step, count)},
                device_id_type=pl.DeviceIdType.MESH,
            )

        each_peer(count, one)

    greet("freq", n_freq, f_me)
    greet("tm", n_tm, t_me)

    def remote(src, dst, sem, step, axis, count, me):
        return pltpu.make_async_remote_copy(
            src_ref=src,
            dst_ref=dst,
            send_sem=sem.at[0, step],
            recv_sem=sem.at[1, step],
            device_id={axis: lax.rem(me + step, count)},
            device_id_type=pl.DeviceIdType.MESH,
        )

    def exchange(buf, tile, sem, axis, count, me):
        buf[me] = tile

        def copy(step):
            return remote(buf.at[me], buf.at[me], sem, step, axis, count, me)

        each_peer(count, lambda step: copy(step).start())
        each_peer(count, lambda step: copy(step).wait_recv())
        total = jnp.sum(buf[...], axis=0)
        each_peer(count, lambda step: copy(step).wait_send())
        return total

    row_ant = lax.rem(lax.broadcasted_iota(jnp.int32, (LANES, baselines), 0), ants)
    hot[:, padded - LANES : padded] = jnp.zeros((LANES, LANES), jnp.bfloat16)
    hot[:, 2 * padded - LANES : 2 * padded] = jnp.zeros((LANES, LANES), jnp.bfloat16)
    hot[:, 0:baselines] = (row_ant == first[...]).astype(jnp.float32).astype(jnp.bfloat16)
    hot[:, padded : padded + baselines] = (
        (row_ant == second[...]).astype(jnp.float32).astype(jnp.bfloat16)
    )

    lane = lax.broadcasted_iota(jnp.int32, (times, LANES), 1)
    row = lax.broadcasted_iota(jnp.int32, (times, LANES), 0)
    lower = lane < ants
    number = jnp.broadcast_to(f_me, (times, LANES)).astype(jnp.float32)
    frequency = (number + 0.5) / channels - 0.5
    turning = FULL_TURN * frequency

    def spread(rows):
        value = jnp.zeros((times, LANES), jnp.float32)
        for i in range(intervals):
            value = jnp.where(row // INTERVAL_TIMES == i, rows[i], value)
        return value

    def stack_rows(rows, height):
        index = lax.broadcasted_iota(jnp.int32, (height, LANES), 0)
        value = jnp.zeros((height, LANES), jnp.float32)
        for i, one in enumerate(rows):
            value = jnp.where(index == i, one, value)
        return value

    def row_of(i):
        return params[i : i + 1, :]

    g_time = tuple(
        spread([row_of(part * intervals + i) for i in range(intervals)]) for part in range(2)
    )
    base = 2 * intervals
    full = (times, LANES)
    g_band = tuple(jnp.broadcast_to(row_of(base + part), full) for part in range(2))
    turns = jnp.broadcast_to(row_of(base + 2), full)

    def chunk(c):
        return slice(c * width, (c + 1) * width)

    def load(ref, c):
        return [
            [(ref[2 * a + b, :, chunk(c)], ref[4 + 2 * a + b, :, chunk(c)]) for b in range(2)]
            for a in range(2)
        ]

    for c in range(chunks):
        v, k = load(vis, c), load(sky, c)
        for a in range(2):
            for b in range(2):
                u = conj_mul(k[a][b], v[a][b])
                u_ref[2 * a + b, :, chunk(c)] = u[0]
                u_ref[4 + 2 * a + b, :, chunk(c)] = u[1]
                q_ref[2 * a + b, :, chunk(c)] = power(k[a][b])

    def chain():
        angle = FULL_TURN * turns * frequency
        phasor = (jnp.cos(angle), jnp.sin(angle))
        band_delay = cmul(g_band, phasor)
        return cmul(g_time, band_delay), band_delay, phasor

    def antenna_rows(g):
        zero = jnp.zeros(full, jnp.float32)
        rows = []
        for part in range(2):
            rows.append(jnp.where(lower, g[part], zero))
            rows.append(jnp.where(lower, zero, g[part]))
        return jnp.concatenate(split3(jnp.concatenate(rows, axis=0)), axis=0)

    def gathered(rows, c, offset):
        got = jnp.dot(
            rows,
            hot[:, offset + c * width : offset + (c + 1) * width],
            preferred_element_type=jnp.float32,
        )
        size = 4 * times
        got = got[0:size] + got[size : 2 * size] + got[2 * size : 3 * size]
        part = [got[i * times : (i + 1) * times] for i in range(4)]
        return [(part[0], part[2]), (part[1], part[3])]

    def both(rows, c):
        return gathered(rows, c, 0), gathered(rows, c, padded)

    def residual_of(c, gp, gq):
        v, k = load(vis, c), load(sky, c)
        result = [[None, None], [None, None]]
        for a in range(2):
            for b in range(2):
                m = conj_mul(gq[b], cmul(gp[a], k[a][b]))
                result[a][b] = (v[a][b][0] - m[0], v[a][b][1] - m[1])
        return result

    def products(c, gp, gq):
        u = load(u_ref, c)
        q = [[q_ref[2 * a + b, :, chunk(c)] for b in range(2)] for a in range(2)]
        pp, pq = [power(x) for x in gp], [power(x) for x in gq]
        lead = [[None] * 2, [None] * 2]
        trail = [[None] * 2, [None] * 2]
        for i in range(2):
            x, y = cmul(u[i][0], gq[0]), cmul(u[i][1], gq[1])
            lead[0][i], lead[1][i] = x[0] + y[0], x[1] + y[1]
            x, y = conj_mul(u[0][i], gp[0]), conj_mul(u[1][i], gp[1])
            trail[0][i], trail[1][i] = x[0] + y[0], x[1] + y[1]
        lead_power = [q[i][0] * pq[0] + q[i][1] * pq[1] for i in range(2)]
        trail_power = [q[0][i] * pp[0] + q[1][i] * pp[1] for i in range(2)]
        return lead[0] + lead[1] + lead_power, trail[0] + trail[1] + trail_power

    def put_terms(c, tiles, offset, weight):
        stacked = jnp.concatenate([weight * tile for tile in tiles], axis=0)
        size = 6 * times
        for i, part in enumerate(split3(stacked)):
            terms[i * size : (i + 1) * size, offset + c * width : offset + (c + 1) * width] = part

    def antenna_sums():
        got = lax.dot_general(
            terms[...],
            hot[...],
            (((1,), (1,)), ((), ())),
            preferred_element_type=jnp.float32,
        )
        size = 6 * times
        got = got[0:size] + got[size : 2 * size] + got[2 * size : 3 * size]
        part = [got[i * times : (i + 1) * times] for i in range(6)]
        return [jnp.where(lower, part[2 * i], part[2 * i + 1]) for i in range(3)]

    def normal(g, weights_at):
        rows = antenna_rows(g)
        for c in range(chunks):
            gp, gq = both(rows, c)
            lead, trail = products(c, gp, gq)
            put_terms(c, lead, 0, weights_at(c))
            put_terms(c, trail, padded, weights_at(c))
        return finish_normal(g)

    def finish_normal(g):
        real, imag, e = antenna_sums()
        return (real - g[0] * e, imag - g[1] * e), e

    def over_times(x):
        return jnp.sum(x, axis=0, keepdims=True)

    owners = chunks
    all_own = owners == n_freq

    def owns(index):
        return True if all_own else index < owners

    for sweep in range(SWEEPS):
        g, band_delay, phasor = chain()
        rows = antenna_rows(g)
        kept = []
        for c in range(chunks):
            gp, gq = both(rows, c)
            r = residual_of(c, gp, gq)
            s_ref[sweep, c] = power(r[0][0]) + power(r[0][1]) + power(r[1][0]) + power(r[1][1])
            kept.append((gp, gq))
        if sweep == 0:
            pl.semaphore_wait(barrier, n_freq - 1 + n_tm - 1)

        def scatter_copy(step):
            peer = lax.rem(f_me + step, n_freq)
            return remote(
                s_ref.at[sweep, peer],
                rs_ref.at[sweep, step],
                rs_sem.at[sweep],
                step,
                "freq",
                n_freq,
                f_me,
            )

        def send_part(step):
            peer = lax.rem(f_me + step, n_freq)
            maybe(owns(peer), lambda: scatter_copy(step).start())

        each_peer(n_freq, send_part)

        for c in range(chunks):
            gp, gq = kept[c]
            lead, trail = products(c, gp, gq)
            for i, tile in enumerate(lead + trail):
                wide[i, :, chunk(c)] = tile

        def own_copy(step):
            return remote(
                w_ref.at[sweep, f_me],
                w_ref.at[sweep, f_me],
                ag_sem.at[sweep],
                step,
                "freq",
                n_freq,
                f_me,
            )

        def reduce_own():
            def arrive(step):
                pltpu.make_async_copy(
                    rs_ref.at[sweep, step], rs_ref.at[sweep, step], rs_sem.at[sweep, 1, step]
                ).wait()

            each_peer(n_freq, arrive)
            total = s_ref[sweep, f_me] + jnp.sum(rs_ref[sweep, 1:n_freq], axis=0)
            w_ref[sweep, f_me] = 1.0 / (total / (4 * channels) + EPSILON)
            each_peer(n_freq, lambda step: own_copy(step).start())

        maybe(owns(f_me), reduce_own)

        def receive_weights(step):
            origin = lax.rem(f_me + n_freq - step, n_freq)

            def arrive():
                pltpu.make_async_copy(
                    w_ref.at[sweep, 0], w_ref.at[sweep, 0], ag_sem.at[sweep, 1, step]
                ).wait()

            maybe(owns(origin), arrive)

        each_peer(n_freq, receive_weights)

        def sent(step):
            peer = lax.rem(f_me + step, n_freq)
            maybe(owns(peer), lambda: scatter_copy(step).wait_send())
            maybe(owns(f_me), lambda: own_copy(step).wait_send())

        each_peer(n_freq, sent)

        for c in range(chunks):
            tiles = [wide[i, :, chunk(c)] for i in range(12)]
            put_terms(c, tiles[:6], 0, w_ref[sweep, c])
            put_terms(c, tiles[6:], padded, w_ref[sweep, c])
        a, e = finish_normal(g)
        n = conj_mul(band_delay, a)
        d = power(band_delay) * e
        rows_out = []
        for value in (n[0], n[1], d):
            for i in range(intervals):
                span = slice(i * INTERVAL_TIMES, (i + 1) * INTERVAL_TIMES)
                rows_out.append(over_times(value[span]))
        tile = stack_rows(rows_out, time_ref.shape[2])
        total = exchange(time_ref.at[sweep], tile, time_sem.at[sweep], "freq", n_freq, f_me)
        part = [total[i : i + 1] for i in range(3 * intervals)]
        g_time = tuple(
            g_time[p]
            + spread(
                [
                    DAMPING * part[p * intervals + i] / part[2 * intervals + i]
                    for i in range(intervals)
                ]
            )
            for p in range(2)
        )

        g, band_delay, phasor = chain()
        a, e = normal(g, lambda c: w_ref[sweep, c])
        other = cmul(g_time, phasor)
        n = conj_mul(other, a)
        tile = stack_rows([over_times(x) for x in (n[0], n[1], power(other) * e)], 8)
        total = exchange(band_ref.at[sweep], tile, band_sem.at[sweep], "tm", n_tm, t_me)
        g_band = tuple(
            g_band[p] + jnp.broadcast_to(DAMPING * total[p : p + 1] / total[2:3], full)
            for p in range(2)
        )

        g, band_delay, phasor = chain()
        a, e = normal(g, lambda c: w_ref[sweep, c])
        n = turning * conj_mul(g, a)[1]
        d = turning * turning * power(g) * e
        tile = stack_rows([over_times(n), over_times(d)], 8)
        tile = exchange(turn_tm_ref.at[sweep], tile, turn_tm_sem.at[sweep], "tm", n_tm, t_me)
        total = exchange(turn_ref.at[sweep], tile, turn_sem.at[sweep], "freq", n_freq, f_me)
        turns = turns + jnp.broadcast_to(DAMPING * total[0:1] / total[1:2], full)

    g, band_delay, phasor = chain()
    rows = antenna_rows(g)
    for c in range(chunks):
        gp, gq = both(rows, c)
        r = residual_of(c, gp, gq)
        stop = min(baselines, (c + 1) * width)
        here = slice(c * width, stop)
        size = stop - c * width
        for i in range(2):
            for a in range(2):
                for b in range(2):
                    out_residual[4 * i + 2 * a + b, :, here] = r[a][b][i][:, :size]
        out_weights[:, here] = w_ref[SWEEPS - 1, c][:, :size]
    rows_out = [
        g_time[p][i * INTERVAL_TIMES : i * INTERVAL_TIMES + 1]
        for p in range(2)
        for i in range(intervals)
    ]
    rows_out += [g_band[0][0:1], g_band[1][0:1], turns[0:1]]
    out_params[...] = stack_rows(rows_out, out_params.shape[0])


def ceil_to(value, step):
    return -(-value // step) * step


def shards(n_freq, n_tm, vis, sky, gain_time, gain_band, delay_start, first, second):
    times, local_channels, baselines = vis.shape[2:]
    antennas = gain_time.shape[-1]
    assert local_channels == 1 and POLS * antennas == LANES
    intervals = times // INTERVAL_TIMES
    channels = local_channels * n_freq
    tiles = -(-baselines // LANES)
    chunks = max(c for c in range(1, min(n_freq, tiles) + 1) if tiles % c == 0)
    width = tiles * LANES // chunks
    padded = tiles * LANES
    margin = ((0, 0), (0, 0), (0, padded - baselines))
    flat = (8, times, baselines)
    count = 2 * intervals + 3
    height = ceil_to(count, 8)
    params = jnp.concatenate(
        [
            gain_time.transpose(0, 2, 1, 3).reshape(2 * intervals, LANES),
            gain_band.transpose(0, 2, 1, 3).reshape(2, LANES),
            delay_start.reshape(1, LANES),
            jnp.zeros((height - count, LANES), jnp.float32),
        ],
        axis=0,
    )
    sizes = (n_freq, n_tm, channels, times, baselines, chunks, width)
    f32 = jnp.float32
    vmem = pl.BlockSpec(memory_space=pltpu.VMEM)
    sems = [
        pltpu.SemaphoreType.DMA((SWEEPS, 2, count))
        for count in (n_freq, n_freq, n_freq, n_tm, n_tm, n_freq)
    ]
    solved, weights, residual = pl.pallas_call(
        functools.partial(kernel, sizes),
        out_shape=(
            jax.ShapeDtypeStruct((height, LANES), f32),
            jax.ShapeDtypeStruct((times, baselines), f32),
            jax.ShapeDtypeStruct(flat, f32),
        ),
        in_specs=[vmem] * 5,
        out_specs=(vmem,) * 3,
        scratch_shapes=[
            pltpu.VMEM((LANES, 2 * padded), jnp.bfloat16),
            pltpu.VMEM((8, times, padded), f32),
            pltpu.VMEM((4, times, padded), f32),
            pltpu.VMEM((12, times, padded), f32),
            pltpu.VMEM((18 * times, 2 * padded), jnp.bfloat16),
            pltpu.VMEM((SWEEPS, chunks, times, width), f32),
            pltpu.VMEM((SWEEPS, n_freq, times, width), f32),
            pltpu.VMEM((SWEEPS, chunks, times, width), f32),
            pltpu.VMEM((SWEEPS, n_freq, ceil_to(3 * intervals, 8), LANES), f32),
            pltpu.VMEM((SWEEPS, n_tm, 8, LANES), f32),
            pltpu.VMEM((SWEEPS, n_tm, 8, LANES), f32),
            pltpu.VMEM((SWEEPS, n_freq, 8, LANES), f32),
            *sems,
        ],
        compiler_params=pltpu.CompilerParams(collective_id=0, has_side_effects=True),
    )(
        jnp.pad(vis.reshape(flat), margin),
        jnp.pad(sky.reshape(flat), margin),
        params,
        first.reshape(1, baselines),
        second.reshape(1, baselines),
    )
    base = 2 * intervals
    solved_time = solved[0:base].reshape(2, intervals, POLS, antennas).transpose(0, 2, 1, 3)
    solved_band = solved[base : base + 2].reshape(2, 1, POLS, antennas).transpose(0, 2, 1, 3)
    solved_delay = solved[base + 2].reshape(POLS, antennas)
    return solved_time, solved_band, solved_delay, weights, residual.reshape(vis.shape)


def solution(mesh):
    in_specs = (
        P(None, None, "tm", "freq", None),
        P(None, None, "tm", "freq", None),
        P(None, None, "tm", None),
        P(None, None, "freq", None),
        P(),
        P(),
        P(),
    )
    out_specs = (
        P(None, None, "tm", None),
        P(None, None, "freq", None),
        P(),
        P("tm", None),
        P(None, None, "tm", "freq", None),
    )
    body = functools.partial(shards, mesh.shape["freq"], mesh.shape["tm"])
    return jax.shard_map(body, mesh=mesh, in_specs=in_specs, out_specs=out_specs, check_vma=False)
```

```python
import functools
import math

import jax
import jax.numpy as jnp
from jax import lax
from jax.experimental import pallas as pl
from jax.experimental.pallas import tpu as pltpu
from jax.sharding import PartitionSpec as P

INTERVAL_TIMES = 4
SWEEPS = 2
FULL_TURN = 2.0 * math.pi
DAMPING = 0.5
EPSILON = 1e-06
LANES = 128
POLS = 2
UNROLLED_PEERS = 8


def cmul(a, b):
    return (a[0] * b[0] - a[1] * b[1], a[0] * b[1] + a[1] * b[0])


def conj_mul(a, b):
    return (a[0] * b[0] + a[1] * b[1], a[0] * b[1] - a[1] * b[0])


def power(a):
    return a[0] * a[0] + a[1] * a[1]


def split3(x):
    high = x.astype(jnp.bfloat16)
    rest = x - high.astype(jnp.float32)
    middle = rest.astype(jnp.bfloat16)
    low = (rest - middle.astype(jnp.float32)).astype(jnp.bfloat16)
    return high, middle, low


def each_peer(count, action):
    if count <= UNROLLED_PEERS:
        for step in range(1, count):
            action(step)
    else:
        lax.fori_loop(1, count, lambda step, carry: (action(step), carry)[1], 0)


def maybe(condition, action):
    if condition is True:
        action()
    else:
        pl.when(condition)(action)


def kernel(
    sizes,
    vis_raw,
    sky_raw,
    gain_time,
    gain_band,
    delay_start,
    first,
    second,
    out_params,
    out_weights,
    out_residual,
    vis,
    sky,
    hot,
    u_ref,
    q_ref,
    wide,
    terms,
    s_ref,
    rs_ref,
    w_ref,
    time_ref,
    band_ref,
    turn_ref,
    rs_sem,
    ag_sem,
    time_sem,
    band_sem,
    turn_sem,
):
    n_freq, n_tm, channels, times, baselines, chunks, width = sizes
    intervals = times // INTERVAL_TIMES
    ants = LANES // POLS
    padded = chunks * width
    f_me = lax.axis_index("freq")
    t_me = lax.axis_index("tm")

    barrier = pltpu.get_barrier_semaphore()

    def each_other(action):
        for across in range(n_tm):
            if across:
                action(across, 0)
            each_peer(n_freq, lambda step: action(across, step))

    def device_at(across, step):
        return {"tm": lax.rem(t_me + across, n_tm), "freq": lax.rem(f_me + step, n_freq)}

    def greet(across, step):
        pl.semaphore_signal(
            barrier,
            inc=1,
            device_id=device_at(across, step),
            device_id_type=pl.DeviceIdType.MESH,
        )

    each_other(greet)

    def remote(src, dst, sem, step, axis, count, me):
        return pltpu.make_async_remote_copy(
            src_ref=src,
            dst_ref=dst,
            send_sem=sem.at[0, step],
            recv_sem=sem.at[1, step],
            device_id={axis: lax.rem(me + step, count)},
            device_id_type=pl.DeviceIdType.MESH,
        )

    def exchange(buf, tile, sem, axis, count, me):
        buf[me] = tile

        def copy(step):
            return remote(buf.at[me], buf.at[me], sem, step, axis, count, me)

        each_peer(count, lambda step: copy(step).start())
        each_peer(count, lambda step: copy(step).wait_recv())
        total = jnp.sum(buf[...], axis=0)
        each_peer(count, lambda step: copy(step).wait_send())
        return total

    def exchange_all(buf, tile, sem):
        buf[t_me, f_me] = tile

        def copy(across, step):
            return pltpu.make_async_remote_copy(
                src_ref=buf.at[t_me, f_me],
                dst_ref=buf.at[t_me, f_me],
                send_sem=sem.at[0, across, step],
                recv_sem=sem.at[1, across, step],
                device_id=device_at(across, step),
                device_id_type=pl.DeviceIdType.MESH,
            )

        each_other(lambda across, step: copy(across, step).start())
        each_other(lambda across, step: copy(across, step).wait_recv())
        total = jnp.sum(jnp.sum(buf[...], axis=0), axis=0)
        each_other(lambda across, step: copy(across, step).wait_send())
        return total

    row_ant = lax.rem(lax.broadcasted_iota(jnp.int32, (LANES, baselines), 0), ants)
    hot[:, padded - LANES : padded] = jnp.zeros((LANES, LANES), jnp.bfloat16)
    hot[:, 2 * padded - LANES : 2 * padded] = jnp.zeros((LANES, LANES), jnp.bfloat16)
    hot[:, 0:baselines] = (row_ant == first[...]).astype(jnp.float32).astype(jnp.bfloat16)
    hot[:, padded : padded + baselines] = (
        (row_ant == second[...]).astype(jnp.float32).astype(jnp.bfloat16)
    )

    lane = lax.broadcasted_iota(jnp.int32, (times, LANES), 1)
    row = lax.broadcasted_iota(jnp.int32, (times, LANES), 0)
    lower = lane < ants
    number = jnp.broadcast_to(f_me, (times, LANES)).astype(jnp.float32)
    frequency = (number + 0.5) / channels - 0.5
    turning = FULL_TURN * frequency

    def spread(rows):
        value = jnp.zeros((times, LANES), jnp.float32)
        for i in range(intervals):
            value = jnp.where(row // INTERVAL_TIMES == i, rows[i], value)
        return value

    def stack_rows(rows, height):
        index = lax.broadcasted_iota(jnp.int32, (height, LANES), 0)
        value = jnp.zeros((height, LANES), jnp.float32)
        for i, one in enumerate(rows):
            value = jnp.where(index == i, one, value)
        return value

    def packed(halves):
        return jnp.concatenate(halves, axis=1)

    full = (times, LANES)
    g_time = tuple(
        spread(
            [
                packed([gain_time[part, p, i : i + 1, :] for p in range(POLS)])
                for i in range(intervals)
            ]
        )
        for part in range(2)
    )
    g_band = tuple(
        jnp.broadcast_to(packed([gain_band[part, p] for p in range(POLS)]), full)
        for part in range(2)
    )
    turns = jnp.broadcast_to(packed([delay_start[p : p + 1, :] for p in range(POLS)]), full)

    def chunk(c):
        return slice(c * width, (c + 1) * width)

    def load(ref, c):
        return [
            [(ref[2 * a + b, :, chunk(c)], ref[4 + 2 * a + b, :, chunk(c)]) for b in range(2)]
            for a in range(2)
        ]

    for raw, ref in ((vis_raw, vis), (sky_raw, sky)):
        for i in range(8):
            ref[i, :, padded - LANES : padded] = jnp.zeros((times, LANES), jnp.float32)
            ref[i, :, 0:baselines] = raw[i // 4, i % 4, :, 0, :]

    for c in range(chunks):
        v, k = load(vis, c), load(sky, c)
        for a in range(2):
            for b in range(2):
                u = conj_mul(k[a][b], v[a][b])
                u_ref[2 * a + b, :, chunk(c)] = u[0]
                u_ref[4 + 2 * a + b, :, chunk(c)] = u[1]
                q_ref[2 * a + b, :, chunk(c)] = power(k[a][b])

    def chain():
        angle = FULL_TURN * turns * frequency
        phasor = (jnp.cos(angle), jnp.sin(angle))
        band_delay = cmul(g_band, phasor)
        return cmul(g_time, band_delay), band_delay, phasor

    def antenna_rows(g):
        zero = jnp.zeros(full, jnp.float32)
        rows = []
        for part in range(2):
            rows.append(jnp.where(lower, g[part], zero))
            rows.append(jnp.where(lower, zero, g[part]))
        return jnp.concatenate(split3(jnp.concatenate(rows, axis=0)), axis=0)

    def gathered(rows, c, offset):
        got = jnp.dot(
            rows,
            hot[:, offset + c * width : offset + (c + 1) * width],
            preferred_element_type=jnp.float32,
        )
        size = 4 * times
        got = got[0:size] + got[size : 2 * size] + got[2 * size : 3 * size]
        part = [got[i * times : (i + 1) * times] for i in range(4)]
        return [(part[0], part[2]), (part[1], part[3])]

    def both(rows, c):
        return gathered(rows, c, 0), gathered(rows, c, padded)

    def residual_of(c, gp, gq):
        v, k = load(vis, c), load(sky, c)
        result = [[None, None], [None, None]]
        for a in range(2):
            for b in range(2):
                m = conj_mul(gq[b], cmul(gp[a], k[a][b]))
                result[a][b] = (v[a][b][0] - m[0], v[a][b][1] - m[1])
        return result

    def products(c, gp, gq):
        u = load(u_ref, c)
        q = [[q_ref[2 * a + b, :, chunk(c)] for b in range(2)] for a in range(2)]
        pp, pq = [power(x) for x in gp], [power(x) for x in gq]
        lead = [[None] * 2, [None] * 2]
        trail = [[None] * 2, [None] * 2]
        for i in range(2):
            x, y = cmul(u[i][0], gq[0]), cmul(u[i][1], gq[1])
            lead[0][i], lead[1][i] = x[0] + y[0], x[1] + y[1]
            x, y = conj_mul(u[0][i], gp[0]), conj_mul(u[1][i], gp[1])
            trail[0][i], trail[1][i] = x[0] + y[0], x[1] + y[1]
        lead_power = [q[i][0] * pq[0] + q[i][1] * pq[1] for i in range(2)]
        trail_power = [q[0][i] * pp[0] + q[1][i] * pp[1] for i in range(2)]
        return lead[0] + lead[1] + lead_power, trail[0] + trail[1] + trail_power

    def put_terms(c, tiles, offset, weight):
        stacked = jnp.concatenate([weight * tile for tile in tiles], axis=0)
        size = 6 * times
        for i, part in enumerate(split3(stacked)):
            terms[i * size : (i + 1) * size, offset + c * width : offset + (c + 1) * width] = part

    def antenna_sums():
        got = lax.dot_general(
            terms[...],
            hot[...],
            (((1,), (1,)), ((), ())),
            preferred_element_type=jnp.float32,
        )
        size = 6 * times
        got = got[0:size] + got[size : 2 * size] + got[2 * size : 3 * size]
        part = [got[i * times : (i + 1) * times] for i in range(6)]
        return [jnp.where(lower, part[2 * i], part[2 * i + 1]) for i in range(3)]

    def normal(g, weights_at):
        rows = antenna_rows(g)
        for c in range(chunks):
            gp, gq = both(rows, c)
            lead, trail = products(c, gp, gq)
            put_terms(c, lead, 0, weights_at(c))
            put_terms(c, trail, padded, weights_at(c))
        return finish_normal(g)

    def finish_normal(g):
        real, imag, e = antenna_sums()
        return (real - g[0] * e, imag - g[1] * e), e

    def over_times(x):
        return jnp.sum(x, axis=0, keepdims=True)

    owners = chunks
    all_own = owners == n_freq

    def owns(index):
        return True if all_own else index < owners

    for sweep in range(SWEEPS):
        g, band_delay, phasor = chain()
        rows = antenna_rows(g)
        kept = []
        for c in range(chunks):
            gp, gq = both(rows, c)
            r = residual_of(c, gp, gq)
            s_ref[sweep, c] = power(r[0][0]) + power(r[0][1]) + power(r[1][0]) + power(r[1][1])
            kept.append((gp, gq))
        if sweep == 0:
            pl.semaphore_wait(barrier, n_freq * n_tm - 1)

        def scatter_copy(step):
            peer = lax.rem(f_me + step, n_freq)
            return remote(
                s_ref.at[sweep, peer],
                rs_ref.at[sweep, step],
                rs_sem.at[sweep],
                step,
                "freq",
                n_freq,
                f_me,
            )

        def send_part(step):
            peer = lax.rem(f_me + step, n_freq)
            maybe(owns(peer), lambda: scatter_copy(step).start())

        each_peer(n_freq, send_part)

        for c in range(chunks):
            gp, gq = kept[c]
            lead, trail = products(c, gp, gq)
            for i, tile in enumerate(lead + trail):
                wide[i, :, chunk(c)] = tile

        def own_copy(step):
            return remote(
                w_ref.at[sweep, f_me],
                w_ref.at[sweep, f_me],
                ag_sem.at[sweep],
                step,
                "freq",
                n_freq,
                f_me,
            )

        def reduce_own():
            def arrive(step):
                pltpu.make_async_copy(
                    rs_ref.at[sweep, step], rs_ref.at[sweep, step], rs_sem.at[sweep, 1, step]
                ).wait()

            each_peer(n_freq, arrive)
            total = s_ref[sweep, f_me] + jnp.sum(rs_ref[sweep, 1:n_freq], axis=0)
            w_ref[sweep, f_me] = 1.0 / (total / (4 * channels) + EPSILON)
            each_peer(n_freq, lambda step: own_copy(step).start())

        maybe(owns(f_me), reduce_own)

        def receive_weights(step):
            origin = lax.rem(f_me + n_freq - step, n_freq)

            def arrive():
                pltpu.make_async_copy(
                    w_ref.at[sweep, 0], w_ref.at[sweep, 0], ag_sem.at[sweep, 1, step]
                ).wait()

            maybe(owns(origin), arrive)

        each_peer(n_freq, receive_weights)

        def sent(step):
            peer = lax.rem(f_me + step, n_freq)
            maybe(owns(peer), lambda: scatter_copy(step).wait_send())
            maybe(owns(f_me), lambda: own_copy(step).wait_send())

        each_peer(n_freq, sent)

        for c in range(chunks):
            tiles = [wide[i, :, chunk(c)] for i in range(12)]
            put_terms(c, tiles[:6], 0, w_ref[sweep, c])
            put_terms(c, tiles[6:], padded, w_ref[sweep, c])
        a, e = finish_normal(g)
        n = conj_mul(band_delay, a)
        d = power(band_delay) * e
        rows_out = []
        for value in (n[0], n[1], d):
            for i in range(intervals):
                span = slice(i * INTERVAL_TIMES, (i + 1) * INTERVAL_TIMES)
                rows_out.append(over_times(value[span]))
        tile = stack_rows(rows_out, time_ref.shape[2])
        total = exchange(time_ref.at[sweep], tile, time_sem.at[sweep], "freq", n_freq, f_me)
        part = [total[i : i + 1] for i in range(3 * intervals)]
        g_time = tuple(
            g_time[p]
            + spread(
                [
                    DAMPING * part[p * intervals + i] / part[2 * intervals + i]
                    for i in range(intervals)
                ]
            )
            for p in range(2)
        )

        g, band_delay, phasor = chain()
        a, e = normal(g, lambda c: w_ref[sweep, c])
        other = cmul(g_time, phasor)
        n = conj_mul(other, a)
        tile = stack_rows([over_times(x) for x in (n[0], n[1], power(other) * e)], 8)
        total = exchange(band_ref.at[sweep], tile, band_sem.at[sweep], "tm", n_tm, t_me)
        g_band = tuple(
            g_band[p] + jnp.broadcast_to(DAMPING * total[p : p + 1] / total[2:3], full)
            for p in range(2)
        )

        g, band_delay, phasor = chain()
        a, e = normal(g, lambda c: w_ref[sweep, c])
        n = turning * conj_mul(g, a)[1]
        d = turning * turning * power(g) * e
        tile = stack_rows([over_times(n), over_times(d)], 2)
        total = exchange_all(turn_ref.at[sweep], tile, turn_sem.at[sweep])
        turns = turns + jnp.broadcast_to(DAMPING * total[0:1] / total[1:2], full)

    g, band_delay, phasor = chain()
    rows = antenna_rows(g)
    for c in range(chunks):
        gp, gq = both(rows, c)
        r = residual_of(c, gp, gq)
        stop = min(baselines, (c + 1) * width)
        here = slice(c * width, stop)
        size = stop - c * width
        for i in range(2):
            for a in range(2):
                for b in range(2):
                    out_residual[4 * i + 2 * a + b, :, here] = r[a][b][i][:, :size]
        out_weights[:, here] = w_ref[SWEEPS - 1, c][:, :size]
    rows_out = [
        g_time[p][i * INTERVAL_TIMES : i * INTERVAL_TIMES + 1]
        for p in range(2)
        for i in range(intervals)
    ]
    rows_out += [g_band[0][0:1], g_band[1][0:1], turns[0:1]]
    out_params[...] = stack_rows(rows_out, out_params.shape[0])


def write_kernel(intervals, params, weights, residual, o_time, o_band, o_delay, o_weights, o_residual):
    ants = LANES // POLS
    for p in range(POLS):
        half = slice(p * ants, (p + 1) * ants)
        for part in range(2):
            o_time[part, p] = params[part * intervals : (part + 1) * intervals, half]
            o_band[part, p] = params[2 * intervals + part : 2 * intervals + part + 1, half]
        o_delay[p : p + 1, :] = params[2 * intervals + 2 : 2 * intervals + 3, half]
    o_weights[...] = weights[...]
    for i in range(8):
        o_residual[i // 4, i % 4, :, 0, :] = residual[i]


def ceil_to(value, step):
    return -(-value // step) * step


def shards(n_freq, n_tm, vis, sky, gain_time, gain_band, delay_start, first, second):
    times, local_channels, baselines = vis.shape[2:]
    antennas = gain_time.shape[-1]
    assert local_channels == 1 and POLS * antennas == LANES
    intervals = times // INTERVAL_TIMES
    channels = local_channels * n_freq
    tiles = -(-baselines // LANES)
    chunks = max(c for c in range(1, min(n_freq, tiles) + 1) if tiles % c == 0)
    width = tiles * LANES // chunks
    padded = tiles * LANES
    flat = (8, times, baselines)
    count = 2 * intervals + 3
    height = ceil_to(count, 8)
    sizes = (n_freq, n_tm, channels, times, baselines, chunks, width)
    f32 = jnp.float32
    vmem = pl.BlockSpec(memory_space=pltpu.VMEM)
    sems = [
        pltpu.SemaphoreType.DMA((SWEEPS, 2) + counts)
        for counts in ((n_freq,), (n_freq,), (n_freq,), (n_tm,), (n_tm, n_freq))
    ]
    solved, weights, residual = pl.pallas_call(
        functools.partial(kernel, sizes),
        out_shape=(
            jax.ShapeDtypeStruct((height, LANES), f32),
            jax.ShapeDtypeStruct((times, baselines), f32),
            jax.ShapeDtypeStruct(flat, f32),
        ),
        in_specs=[vmem] * 7,
        out_specs=(vmem,) * 3,
        scratch_shapes=[
            pltpu.VMEM((8, times, padded), f32),
            pltpu.VMEM((8, times, padded), f32),
            pltpu.VMEM((LANES, 2 * padded), jnp.bfloat16),
            pltpu.VMEM((8, times, padded), f32),
            pltpu.VMEM((4, times, padded), f32),
            pltpu.VMEM((12, times, padded), f32),
            pltpu.VMEM((18 * times, 2 * padded), jnp.bfloat16),
            pltpu.VMEM((SWEEPS, chunks, times, width), f32),
            pltpu.VMEM((SWEEPS, n_freq, times, width), f32),
            pltpu.VMEM((SWEEPS, chunks, times, width), f32),
            pltpu.VMEM((SWEEPS, n_freq, ceil_to(3 * intervals, 8), LANES), f32),
            pltpu.VMEM((SWEEPS, n_tm, 8, LANES), f32),
            pltpu.VMEM((SWEEPS, n_tm, n_freq, 2, LANES), f32),
            *sems,
        ],
        compiler_params=pltpu.CompilerParams(collective_id=0, has_side_effects=True),
    )(
        vis,
        sky,
        gain_time,
        gain_band,
        delay_start,
        first.reshape(1, baselines),
        second.reshape(1, baselines),
    )
    return pl.pallas_call(
        functools.partial(write_kernel, intervals),
        out_shape=tuple(
            jax.ShapeDtypeStruct(like.shape, f32)
            for like in (gain_time, gain_band, delay_start, weights, vis)
        ),
        in_specs=[vmem] * 3,
        out_specs=(vmem,) * 5,
    )(solved, weights, residual)


def solution(mesh):
    in_specs = (
        P(None, None, "tm", "freq", None),
        P(None, None, "tm", "freq", None),
        P(None, None, "tm", None),
        P(None, None, "freq", None),
        P(),
        P(),
        P(),
    )
    out_specs = (
        P(None, None, "tm", None),
        P(None, None, "freq", None),
        P(),
        P("tm", None),
        P(None, None, "tm", "freq", None),
    )
    body = functools.partial(shards, mesh.shape["freq"], mesh.shape["tm"])
    return jax.shard_map(body, mesh=mesh, in_specs=in_specs, out_specs=out_specs, check_vma=False)
```

```python
import functools
import math

import jax
import jax.numpy as jnp
from jax import lax
from jax.experimental import pallas as pl
from jax.experimental.pallas import tpu as pltpu
from jax.sharding import PartitionSpec as P

INTERVAL_TIMES = 4
SWEEPS = 2
FULL_TURN = 2.0 * math.pi
DAMPING = 0.5
EPSILON = 1e-06
LANES = 128
POLS = 2
UNROLLED_PEERS = 8


def cmul(a, b):
    return (a[0] * b[0] - a[1] * b[1], a[0] * b[1] + a[1] * b[0])


def conj_mul(a, b):
    return (a[0] * b[0] + a[1] * b[1], a[0] * b[1] - a[1] * b[0])


def power(a):
    return a[0] * a[0] + a[1] * a[1]


def split3(x):
    high = x.astype(jnp.bfloat16)
    rest = x - high.astype(jnp.float32)
    middle = rest.astype(jnp.bfloat16)
    low = (rest - middle.astype(jnp.float32)).astype(jnp.bfloat16)
    return high, middle, low


def each_peer(count, action):
    if count <= UNROLLED_PEERS:
        for step in range(1, count):
            action(step)
    else:
        lax.fori_loop(1, count, lambda step, carry: (action(step), carry)[1], 0)


def maybe(condition, action):
    if condition is True:
        action()
    else:
        pl.when(condition)(action)


def kernel(
    sizes,
    vis_raw,
    sky_raw,
    gain_time,
    gain_band,
    delay_start,
    first,
    second,
    out_params,
    out_weights,
    out_residual,
    vis,
    sky,
    hot,
    u_ref,
    q_ref,
    c_ref,
    g_ref,
    terms,
    s_ref,
    rs_ref,
    w_ref,
    time_ref,
    band_ref,
    turn_ref,
    rs_sem,
    ag_sem,
    time_sem,
    band_sem,
    turn_sem,
):
    n_freq, n_tm, channels, times, baselines, chunks, width = sizes
    intervals = times // INTERVAL_TIMES
    ants = LANES // POLS
    padded = chunks * width
    f_me = lax.axis_index("freq")
    t_me = lax.axis_index("tm")

    barrier = pltpu.get_barrier_semaphore()

    def each_other(action):
        for across in range(n_tm):
            if across:
                action(across, 0)
            each_peer(n_freq, lambda step: action(across, step))

    def device_at(across, step):
        return {"tm": lax.rem(t_me + across, n_tm), "freq": lax.rem(f_me + step, n_freq)}

    def greet(across, step):
        pl.semaphore_signal(
            barrier,
            inc=1,
            device_id=device_at(across, step),
            device_id_type=pl.DeviceIdType.MESH,
        )

    each_other(greet)

    def remote(src, dst, sem, step, axis, count, me):
        return pltpu.make_async_remote_copy(
            src_ref=src,
            dst_ref=dst,
            send_sem=sem.at[0, step],
            recv_sem=sem.at[1, step],
            device_id={axis: lax.rem(me + step, count)},
            device_id_type=pl.DeviceIdType.MESH,
        )

    def exchange(buf, tile, sem, axis, count, me):
        buf[me] = tile

        def copy(step):
            return remote(buf.at[me], buf.at[me], sem, step, axis, count, me)

        each_peer(count, lambda step: copy(step).start())
        each_peer(count, lambda step: copy(step).wait_recv())
        total = jnp.sum(buf[...], axis=0)
        each_peer(count, lambda step: copy(step).wait_send())
        return total

    def exchange_all(buf, tile, sem):
        buf[t_me, f_me] = tile

        def copy(across, step):
            return pltpu.make_async_remote_copy(
                src_ref=buf.at[t_me, f_me],
                dst_ref=buf.at[t_me, f_me],
                send_sem=sem.at[0, across, step],
                recv_sem=sem.at[1, across, step],
                device_id=device_at(across, step),
                device_id_type=pl.DeviceIdType.MESH,
            )

        each_other(lambda across, step: copy(across, step).start())
        each_other(lambda across, step: copy(across, step).wait_recv())
        total = jnp.sum(jnp.sum(buf[...], axis=0), axis=0)
        each_other(lambda across, step: copy(across, step).wait_send())
        return total

    row_ant = lax.rem(lax.broadcasted_iota(jnp.int32, (LANES, baselines), 0), ants)
    hot[:, padded - LANES : padded] = jnp.zeros((LANES, LANES), jnp.bfloat16)
    hot[:, 2 * padded - LANES : 2 * padded] = jnp.zeros((LANES, LANES), jnp.bfloat16)
    hot[:, 0:baselines] = (row_ant == first[...]).astype(jnp.float32).astype(jnp.bfloat16)
    hot[:, padded : padded + baselines] = (
        (row_ant == second[...]).astype(jnp.float32).astype(jnp.bfloat16)
    )

    lane = lax.broadcasted_iota(jnp.int32, (times, LANES), 1)
    row = lax.broadcasted_iota(jnp.int32, (times, LANES), 0)
    lower = lane < ants
    number = jnp.broadcast_to(f_me, (times, LANES)).astype(jnp.float32)
    frequency = (number + 0.5) / channels - 0.5
    turning = FULL_TURN * frequency

    def spread(rows):
        value = jnp.zeros((times, LANES), jnp.float32)
        for i in range(intervals):
            value = jnp.where(row // INTERVAL_TIMES == i, rows[i], value)
        return value

    def stack_rows(rows, height):
        index = lax.broadcasted_iota(jnp.int32, (height, LANES), 0)
        value = jnp.zeros((height, LANES), jnp.float32)
        for i, one in enumerate(rows):
            value = jnp.where(index == i, one, value)
        return value

    def packed(halves):
        return jnp.concatenate(halves, axis=1)

    full = (times, LANES)
    g_time = tuple(
        spread(
            [
                packed([gain_time[part, p, i : i + 1, :] for p in range(POLS)])
                for i in range(intervals)
            ]
        )
        for part in range(2)
    )
    g_band = tuple(
        jnp.broadcast_to(packed([gain_band[part, p] for p in range(POLS)]), full)
        for part in range(2)
    )
    turns = jnp.broadcast_to(packed([delay_start[p : p + 1, :] for p in range(POLS)]), full)

    def chunk(c):
        return slice(c * width, (c + 1) * width)

    def load(ref, c):
        return [
            [(ref[2 * a + b, :, chunk(c)], ref[4 + 2 * a + b, :, chunk(c)]) for b in range(2)]
            for a in range(2)
        ]

    for raw, ref in ((vis_raw, vis), (sky_raw, sky)):
        for i in range(8):
            ref[i, :, padded - LANES : padded] = jnp.zeros((times, LANES), jnp.float32)
            ref[i, :, 0:baselines] = raw[i // 4, i % 4, :, 0, :]

    for c in range(chunks):
        v, k = load(vis, c), load(sky, c)
        for a in range(2):
            for b in range(2):
                u = conj_mul(k[a][b], v[a][b])
                u_ref[2 * a + b, :, chunk(c)] = u[0]
                u_ref[4 + 2 * a + b, :, chunk(c)] = u[1]
                q_ref[2 * a + b, :, chunk(c)] = power(k[a][b])

    def chain():
        angle = FULL_TURN * turns * frequency
        phasor = (jnp.cos(angle), jnp.sin(angle))
        band_delay = cmul(g_band, phasor)
        return cmul(g_time, band_delay), band_delay, phasor

    def antenna_rows(g):
        zero = jnp.zeros(full, jnp.float32)
        rows = []
        for part in range(2):
            rows.append(jnp.where(lower, g[part], zero))
            rows.append(jnp.where(lower, zero, g[part]))
        return jnp.concatenate(split3(jnp.concatenate(rows, axis=0)), axis=0)

    def gathered(rows, c, offset):
        got = jnp.dot(
            rows,
            hot[:, offset + c * width : offset + (c + 1) * width],
            preferred_element_type=jnp.float32,
        )
        size = 4 * times
        got = got[0:size] + got[size : 2 * size] + got[2 * size : 3 * size]
        part = [got[i * times : (i + 1) * times] for i in range(4)]
        return [(part[0], part[2]), (part[1], part[3])]

    def both(rows, c):
        return gathered(rows, c, 0), gathered(rows, c, padded)

    def residual_of(c, gp, gq):
        v, k = load(vis, c), load(sky, c)
        result = [[None, None], [None, None]]
        for a in range(2):
            for b in range(2):
                m = conj_mul(gq[b], cmul(gp[a], k[a][b]))
                result[a][b] = (v[a][b][0] - m[0], v[a][b][1] - m[1])
        return result

    own_mask = (lane // ants) == lax.rem(row // 2, 2)
    other_mask = (lane // ants) == lax.rem(row, 2)
    wide_row = lax.rem(lax.broadcasted_iota(jnp.int32, (times, width), 0), INTERVAL_TIMES)

    def fold(v):
        even = lax.rem(wide_row, 2) == 0
        pair = [
            jnp.where(
                even,
                v[k] + pltpu.roll(v[k], times - 1, 0),
                v[k + 1] + pltpu.roll(v[k + 1], 1, 0),
            )
            for k in (0, 2)
        ]
        return jnp.where(
            wide_row < 2,
            pair[0] + pltpu.roll(pair[0], times - 2, 0),
            pair[1] + pltpu.roll(pair[1], 2, 0),
        )

    def swap(x):
        return jnp.where(
            wide_row == 1,
            pltpu.roll(x, times - 1, 0),
            jnp.where(wide_row == 2, pltpu.roll(x, 1, 0), x),
        )

    def put_matrices(c, weight):
        lead = slice(c * width, (c + 1) * width)
        trail = slice(padded + c * width, padded + (c + 1) * width)
        folded = [
            fold([weight * source[base + k, :, lead] for k in range(4)])
            for source, base in ((u_ref, 0), (u_ref, 4), (q_ref, 0))
        ]
        for i, value in enumerate(folded):
            c_ref[i, :, lead] = value
            turned = swap(value)
            c_ref[i, :, trail] = -turned if i == 1 else turned

    def gather_others(g):
        zero = jnp.zeros(full, jnp.float32)
        rows = jnp.concatenate([jnp.where(other_mask, x, zero) for x in g], axis=0)
        rows = jnp.concatenate(split3(rows), axis=0)
        size = 2 * times
        for k in range(2 * chunks):
            source = ((k + chunks) % (2 * chunks)) * width
            got = jnp.dot(
                rows, hot[:, source : source + width], preferred_element_type=jnp.float32
            )
            got = got[0:size] + got[size : 2 * size] + got[2 * size : 3 * size]
            g_ref[0, :, k * width : (k + 1) * width] = got[:times]
            g_ref[1, :, k * width : (k + 1) * width] = got[times:]

    def normal(g):
        for k in range(2 * chunks):
            here = slice(k * width, (k + 1) * width)
            m = (c_ref[0, :, here], c_ref[1, :, here])
            y = (g_ref[0, :, here], g_ref[1, :, here])
            x = cmul(m, y)
            parts = [[], [], []]
            for tile in (x[0], x[1], c_ref[2, :, here] * power(y)):
                high = tile.astype(jnp.bfloat16).astype(jnp.float32)
                rest = tile - high
                middle = rest.astype(jnp.bfloat16).astype(jnp.float32)
                for part, value in zip(parts, (high, middle, rest - middle)):
                    part.append(value)
            filler = [jnp.zeros((times, width), jnp.float32)]
            stacked = jnp.concatenate(parts[0] + parts[1] + parts[2] + filler, axis=0)
            terms[:, here] = stacked.astype(jnp.bfloat16)
        got = lax.dot_general(
            terms[...],
            hot[...],
            (((1,), (1,)), ((), ())),
            preferred_element_type=jnp.float32,
        )
        size = 3 * times
        got = got[0:size] + got[size : 2 * size] + got[2 * size : 3 * size]
        zero = jnp.zeros(full, jnp.float32)
        real, imag, e = [
            jnp.where(own_mask, got[i * times : (i + 1) * times], zero) for i in range(3)
        ]
        return (real - g[0] * e, imag - g[1] * e), e

    def over_times(x):
        return jnp.sum(x, axis=0, keepdims=True)

    owners = chunks
    all_own = owners == n_freq

    def owns(index):
        return True if all_own else index < owners

    for sweep in range(SWEEPS):
        g, band_delay, phasor = chain()
        rows = antenna_rows(g)
        for c in range(chunks):
            gp, gq = both(rows, c)
            r = residual_of(c, gp, gq)
            s_ref[sweep, c] = power(r[0][0]) + power(r[0][1]) + power(r[1][0]) + power(r[1][1])
        if sweep == 0:
            pl.semaphore_wait(barrier, n_freq * n_tm - 1)

        def scatter_copy(step):
            peer = lax.rem(f_me + step, n_freq)
            return remote(
                s_ref.at[sweep, peer],
                rs_ref.at[sweep, step],
                rs_sem.at[sweep],
                step,
                "freq",
                n_freq,
                f_me,
            )

        def send_part(step):
            peer = lax.rem(f_me + step, n_freq)
            maybe(owns(peer), lambda: scatter_copy(step).start())

        each_peer(n_freq, send_part)

        gather_others(g)

        def own_copy(step):
            return remote(
                w_ref.at[sweep, f_me],
                w_ref.at[sweep, f_me],
                ag_sem.at[sweep],
                step,
                "freq",
                n_freq,
                f_me,
            )

        def reduce_own():
            def arrive(step):
                pltpu.make_async_copy(
                    rs_ref.at[sweep, step], rs_ref.at[sweep, step], rs_sem.at[sweep, 1, step]
                ).wait()

            each_peer(n_freq, arrive)
            total = s_ref[sweep, f_me] + jnp.sum(rs_ref[sweep, 1:n_freq], axis=0)
            w_ref[sweep, f_me] = 1.0 / (total / (4 * channels) + EPSILON)
            each_peer(n_freq, lambda step: own_copy(step).start())

        maybe(owns(f_me), reduce_own)

        def receive_weights(step):
            origin = lax.rem(f_me + n_freq - step, n_freq)

            def arrive():
                pltpu.make_async_copy(
                    w_ref.at[sweep, 0], w_ref.at[sweep, 0], ag_sem.at[sweep, 1, step]
                ).wait()

            maybe(owns(origin), arrive)

        each_peer(n_freq, receive_weights)

        def sent(step):
            peer = lax.rem(f_me + step, n_freq)
            maybe(owns(peer), lambda: scatter_copy(step).wait_send())
            maybe(owns(f_me), lambda: own_copy(step).wait_send())

        each_peer(n_freq, sent)

        for c in range(chunks):
            put_matrices(c, w_ref[sweep, c])
        a, e = normal(g)
        n = conj_mul(band_delay, a)
        d = power(band_delay) * e
        rows_out = []
        for value in (n[0], n[1], d):
            for i in range(intervals):
                span = slice(i * INTERVAL_TIMES, (i + 1) * INTERVAL_TIMES)
                rows_out.append(over_times(value[span]))
        tile = stack_rows(rows_out, time_ref.shape[2])
        total = exchange(time_ref.at[sweep], tile, time_sem.at[sweep], "freq", n_freq, f_me)
        part = [total[i : i + 1] for i in range(3 * intervals)]
        g_time = tuple(
            g_time[p]
            + spread(
                [
                    DAMPING * part[p * intervals + i] / part[2 * intervals + i]
                    for i in range(intervals)
                ]
            )
            for p in range(2)
        )

        g, band_delay, phasor = chain()
        gather_others(g)
        a, e = normal(g)
        other = cmul(g_time, phasor)
        n = conj_mul(other, a)
        tile = stack_rows([over_times(x) for x in (n[0], n[1], power(other) * e)], 8)
        total = exchange(band_ref.at[sweep], tile, band_sem.at[sweep], "tm", n_tm, t_me)
        g_band = tuple(
            g_band[p] + jnp.broadcast_to(DAMPING * total[p : p + 1] / total[2:3], full)
            for p in range(2)
        )

        g, band_delay, phasor = chain()
        gather_others(g)
        a, e = normal(g)
        n = turning * conj_mul(g, a)[1]
        d = turning * turning * power(g) * e
        tile = stack_rows([over_times(n), over_times(d)], 2)
        total = exchange_all(turn_ref.at[sweep], tile, turn_sem.at[sweep])
        turns = turns + jnp.broadcast_to(DAMPING * total[0:1] / total[1:2], full)

    g, band_delay, phasor = chain()
    rows = antenna_rows(g)
    for c in range(chunks):
        gp, gq = both(rows, c)
        r = residual_of(c, gp, gq)
        stop = min(baselines, (c + 1) * width)
        here = slice(c * width, stop)
        size = stop - c * width
        for i in range(2):
            for a in range(2):
                for b in range(2):
                    out_residual[4 * i + 2 * a + b, :, here] = r[a][b][i][:, :size]
        out_weights[:, here] = w_ref[SWEEPS - 1, c][:, :size]
    rows_out = [
        g_time[p][i * INTERVAL_TIMES : i * INTERVAL_TIMES + 1]
        for p in range(2)
        for i in range(intervals)
    ]
    rows_out += [g_band[0][0:1], g_band[1][0:1], turns[0:1]]
    out_params[...] = stack_rows(rows_out, out_params.shape[0])


def write_kernel(intervals, params, weights, residual, o_time, o_band, o_delay, o_weights, o_residual):
    ants = LANES // POLS
    for p in range(POLS):
        half = slice(p * ants, (p + 1) * ants)
        for part in range(2):
            o_time[part, p] = params[part * intervals : (part + 1) * intervals, half]
            o_band[part, p] = params[2 * intervals + part : 2 * intervals + part + 1, half]
        o_delay[p : p + 1, :] = params[2 * intervals + 2 : 2 * intervals + 3, half]
    o_weights[...] = weights[...]
    for i in range(8):
        o_residual[i // 4, i % 4, :, 0, :] = residual[i]


def ceil_to(value, step):
    return -(-value // step) * step


def shards(n_freq, n_tm, vis, sky, gain_time, gain_band, delay_start, first, second):
    times, local_channels, baselines = vis.shape[2:]
    antennas = gain_time.shape[-1]
    assert local_channels == 1 and POLS * antennas == LANES
    intervals = times // INTERVAL_TIMES
    assert times == 8 and INTERVAL_TIMES == POLS * POLS
    channels = local_channels * n_freq
    tiles = -(-baselines // LANES)
    chunks = max(c for c in range(1, min(n_freq, tiles) + 1) if tiles % c == 0)
    width = tiles * LANES // chunks
    padded = tiles * LANES
    flat = (8, times, baselines)
    count = 2 * intervals + 3
    height = ceil_to(count, 8)
    sizes = (n_freq, n_tm, channels, times, baselines, chunks, width)
    f32 = jnp.float32
    vmem = pl.BlockSpec(memory_space=pltpu.VMEM)
    sems = [
        pltpu.SemaphoreType.DMA((SWEEPS, 2) + counts)
        for counts in ((n_freq,), (n_freq,), (n_freq,), (n_tm,), (n_tm, n_freq))
    ]
    solved, weights, residual = pl.pallas_call(
        functools.partial(kernel, sizes),
        out_shape=(
            jax.ShapeDtypeStruct((height, LANES), f32),
            jax.ShapeDtypeStruct((times, baselines), f32),
            jax.ShapeDtypeStruct(flat, f32),
        ),
        in_specs=[vmem] * 7,
        out_specs=(vmem,) * 3,
        scratch_shapes=[
            pltpu.VMEM((8, times, padded), f32),
            pltpu.VMEM((8, times, padded), f32),
            pltpu.VMEM((LANES, 2 * padded), jnp.bfloat16),
            pltpu.VMEM((8, times, padded), f32),
            pltpu.VMEM((4, times, padded), f32),
            pltpu.VMEM((3, times, 2 * padded), f32),
            pltpu.VMEM((2, times, 2 * padded), f32),
            pltpu.VMEM((10 * times, 2 * padded), jnp.bfloat16),
            pltpu.VMEM((SWEEPS, chunks, times, width), f32),
            pltpu.VMEM((SWEEPS, n_freq, times, width), f32),
            pltpu.VMEM((SWEEPS, chunks, times, width), f32),
            pltpu.VMEM((SWEEPS, n_freq, ceil_to(3 * intervals, 8), LANES), f32),
            pltpu.VMEM((SWEEPS, n_tm, 8, LANES), f32),
            pltpu.VMEM((SWEEPS, n_tm, n_freq, 2, LANES), f32),
            *sems,
        ],
        compiler_params=pltpu.CompilerParams(collective_id=0, has_side_effects=True),
    )(
        vis,
        sky,
        gain_time,
        gain_band,
        delay_start,
        first.reshape(1, baselines),
        second.reshape(1, baselines),
    )
    return pl.pallas_call(
        functools.partial(write_kernel, intervals),
        out_shape=tuple(
            jax.ShapeDtypeStruct(like.shape, f32)
            for like in (gain_time, gain_band, delay_start, weights, vis)
        ),
        in_specs=[vmem] * 3,
        out_specs=(vmem,) * 5,
    )(solved, weights, residual)


def solution(mesh):
    in_specs = (
        P(None, None, "tm", "freq", None),
        P(None, None, "tm", "freq", None),
        P(None, None, "tm", None),
        P(None, None, "freq", None),
        P(),
        P(),
        P(),
    )
    out_specs = (
        P(None, None, "tm", None),
        P(None, None, "freq", None),
        P(),
        P("tm", None),
        P(None, None, "tm", "freq", None),
    )
    body = functools.partial(shards, mesh.shape["freq"], mesh.shape["tm"])
    return jax.shard_map(body, mesh=mesh, in_specs=in_specs, out_specs=out_specs, check_vma=False)
```

```python
import functools
import math

import jax
import jax.numpy as jnp
from jax import lax
from jax.experimental import pallas as pl
from jax.experimental.pallas import tpu as pltpu
from jax.sharding import PartitionSpec as P

INTERVAL_TIMES = 4
SWEEPS = 2
FULL_TURN = 2.0 * math.pi
DAMPING = 0.5
EPSILON = 1e-06
LANES = 128
POLS = 2
UNROLLED_PEERS = 8


def cmul(a, b):
    return (a[0] * b[0] - a[1] * b[1], a[0] * b[1] + a[1] * b[0])


def conj_mul(a, b):
    return (a[0] * b[0] + a[1] * b[1], a[0] * b[1] - a[1] * b[0])


def power(a):
    return a[0] * a[0] + a[1] * a[1]


def split3(x):
    high = x.astype(jnp.bfloat16)
    rest = x - high.astype(jnp.float32)
    middle = rest.astype(jnp.bfloat16)
    low = (rest - middle.astype(jnp.float32)).astype(jnp.bfloat16)
    return high, middle, low


def each_peer(count, action):
    if count <= UNROLLED_PEERS:
        for step in range(1, count):
            action(step)
    else:
        lax.fori_loop(1, count, lambda step, carry: (action(step), carry)[1], 0)


def maybe(condition, action):
    if condition is True:
        action()
    else:
        pl.when(condition)(action)


def kernel(
    sizes,
    vis_arg,
    sky_arg,
    gain_time,
    gain_band,
    delay_start,
    first,
    second,
    out_params,
    out_weights,
    out_residual,
    vis_raw,
    sky_raw,
    raw_sem,
    vis,
    sky,
    hot,
    u_ref,
    q_ref,
    c_ref,
    g_ref,
    terms,
    s_ref,
    rs_ref,
    w_ref,
    time_ref,
    band_ref,
    turn_ref,
    rs_sem,
    ag_sem,
    time_sem,
    band_sem,
    turn_sem,
):
    n_freq, n_tm, channels, times, baselines, chunks, width = sizes
    intervals = times // INTERVAL_TIMES
    ants = LANES // POLS
    padded = chunks * width
    f_me = lax.axis_index("freq")
    t_me = lax.axis_index("tm")

    barrier = pltpu.get_barrier_semaphore()

    def each_other(action):
        for across in range(n_tm):
            if across:
                action(across, 0)
            each_peer(n_freq, lambda step: action(across, step))

    def device_at(across, step):
        return {"tm": lax.rem(t_me + across, n_tm), "freq": lax.rem(f_me + step, n_freq)}

    def greet(across, step):
        pl.semaphore_signal(
            barrier,
            inc=1,
            device_id=device_at(across, step),
            device_id_type=pl.DeviceIdType.MESH,
        )

    each_other(greet)
    fetches = [
        pltpu.make_async_copy(source, target, raw_sem.at[i])
        for i, (source, target) in enumerate(((vis_arg, vis_raw), (sky_arg, sky_raw)))
    ]
    for fetch in fetches:
        fetch.start()

    def remote(src, dst, sem, step, axis, count, me):
        return pltpu.make_async_remote_copy(
            src_ref=src,
            dst_ref=dst,
            send_sem=sem.at[0, step],
            recv_sem=sem.at[1, step],
            device_id={axis: lax.rem(me + step, count)},
            device_id_type=pl.DeviceIdType.MESH,
        )

    def exchange(buf, tile, sem, axis, count, me):
        buf[me] = tile

        def copy(step):
            return remote(buf.at[me], buf.at[me], sem, step, axis, count, me)

        each_peer(count, lambda step: copy(step).start())
        each_peer(count, lambda step: copy(step).wait_recv())
        total = jnp.sum(buf[...], axis=0)
        each_peer(count, lambda step: copy(step).wait_send())
        return total

    def exchange_all(buf, tile, sem):
        buf[t_me, f_me] = tile

        def copy(across, step):
            return pltpu.make_async_remote_copy(
                src_ref=buf.at[t_me, f_me],
                dst_ref=buf.at[t_me, f_me],
                send_sem=sem.at[0, across, step],
                recv_sem=sem.at[1, across, step],
                device_id=device_at(across, step),
                device_id_type=pl.DeviceIdType.MESH,
            )

        each_other(lambda across, step: copy(across, step).start())
        each_other(lambda across, step: copy(across, step).wait_recv())
        total = jnp.sum(jnp.sum(buf[...], axis=0), axis=0)
        each_other(lambda across, step: copy(across, step).wait_send())
        return total

    row_ant = lax.broadcasted_iota(jnp.int32, (ants, baselines), 0)
    hot[:, padded - LANES : padded] = jnp.zeros((ants, LANES), jnp.bfloat16)
    hot[:, 2 * padded - LANES : 2 * padded] = jnp.zeros((ants, LANES), jnp.bfloat16)
    hot[:, 0:baselines] = (row_ant == first[...]).astype(jnp.float32).astype(jnp.bfloat16)
    hot[:, padded : padded + baselines] = (
        (row_ant == second[...]).astype(jnp.float32).astype(jnp.bfloat16)
    )

    lane = lax.broadcasted_iota(jnp.int32, (times, LANES), 1)
    row = lax.broadcasted_iota(jnp.int32, (times, LANES), 0)
    number = jnp.broadcast_to(f_me, (times, LANES)).astype(jnp.float32)
    frequency = (number + 0.5) / channels - 0.5
    turning = FULL_TURN * frequency

    def spread(rows):
        value = jnp.zeros((times, LANES), jnp.float32)
        for i in range(intervals):
            value = jnp.where(row // INTERVAL_TIMES == i, rows[i], value)
        return value

    def stack_rows(rows, height):
        index = lax.broadcasted_iota(jnp.int32, (height, LANES), 0)
        value = jnp.zeros((height, LANES), jnp.float32)
        for i, one in enumerate(rows):
            value = jnp.where(index == i, one, value)
        return value

    def packed(halves):
        return jnp.concatenate(halves, axis=1)

    full = (times, LANES)
    g_time = tuple(
        spread(
            [
                packed([gain_time[part, p, i : i + 1, :] for p in range(POLS)])
                for i in range(intervals)
            ]
        )
        for part in range(2)
    )
    g_band = tuple(
        jnp.broadcast_to(packed([gain_band[part, p] for p in range(POLS)]), full)
        for part in range(2)
    )
    turns = jnp.broadcast_to(packed([delay_start[p : p + 1, :] for p in range(POLS)]), full)

    def chunk(c):
        return slice(c * width, (c + 1) * width)

    def load(ref, c):
        return [
            [(ref[2 * a + b, :, chunk(c)], ref[4 + 2 * a + b, :, chunk(c)]) for b in range(2)]
            for a in range(2)
        ]

    for fetch, raw, ref in zip(fetches, (vis_raw, sky_raw), (vis, sky)):
        fetch.wait()
        for i in range(8):
            ref[i, :, padded - LANES : padded] = jnp.zeros((times, LANES), jnp.float32)
            ref[i, :, 0:baselines] = raw[i // 4, i % 4, :, 0, :]

    for c in range(chunks):
        v, k = load(vis, c), load(sky, c)
        for a in range(2):
            for b in range(2):
                u = conj_mul(k[a][b], v[a][b])
                u_ref[2 * a + b, :, chunk(c)] = u[0]
                u_ref[4 + 2 * a + b, :, chunk(c)] = u[1]
                q_ref[2 * a + b, :, chunk(c)] = power(k[a][b])

    def chain():
        angle = FULL_TURN * turns * frequency
        phasor = (jnp.cos(angle), jnp.sin(angle))
        band_delay = cmul(g_band, phasor)
        return cmul(g_time, band_delay), band_delay, phasor

    def antenna_rows(g):
        rows = []
        for part in range(2):
            rows.append(g[part][:, :ants])
            rows.append(g[part][:, ants:])
        return jnp.concatenate(split3(jnp.concatenate(rows, axis=0)), axis=0)

    def gathered(rows, c, offset):
        got = jnp.dot(
            rows,
            hot[:, offset + c * width : offset + (c + 1) * width],
            preferred_element_type=jnp.float32,
        )
        size = 4 * times
        got = got[0:size] + got[size : 2 * size] + got[2 * size : 3 * size]
        part = [got[i * times : (i + 1) * times] for i in range(4)]
        return [(part[0], part[2]), (part[1], part[3])]

    def both(rows, c):
        return gathered(rows, c, 0), gathered(rows, c, padded)

    def residual_of(c, gp, gq):
        v, k = load(vis, c), load(sky, c)
        result = [[None, None], [None, None]]
        for a in range(2):
            for b in range(2):
                m = conj_mul(gq[b], cmul(gp[a], k[a][b]))
                result[a][b] = (v[a][b][0] - m[0], v[a][b][1] - m[1])
        return result

    own_mask = (lane // ants) == lax.rem(row // 2, 2)
    other_mask = (lane // ants) == lax.rem(row, 2)
    wide_row = lax.rem(lax.broadcasted_iota(jnp.int32, (times, width), 0), INTERVAL_TIMES)

    def fold(v):
        even = lax.rem(wide_row, 2) == 0
        pair = [
            jnp.where(
                even,
                v[k] + pltpu.roll(v[k], times - 1, 0),
                v[k + 1] + pltpu.roll(v[k + 1], 1, 0),
            )
            for k in (0, 2)
        ]
        return jnp.where(
            wide_row < 2,
            pair[0] + pltpu.roll(pair[0], times - 2, 0),
            pair[1] + pltpu.roll(pair[1], 2, 0),
        )

    def swap(x):
        return jnp.where(
            wide_row == 1,
            pltpu.roll(x, times - 1, 0),
            jnp.where(wide_row == 2, pltpu.roll(x, 1, 0), x),
        )

    def put_matrices(c, weight):
        lead = slice(c * width, (c + 1) * width)
        trail = slice(padded + c * width, padded + (c + 1) * width)
        folded = [
            fold([weight * source[base + k, :, lead] for k in range(4)])
            for source, base in ((u_ref, 0), (u_ref, 4), (q_ref, 0))
        ]
        for i, value in enumerate(folded):
            c_ref[i, :, lead] = value
            turned = swap(value)
            c_ref[i, :, trail] = -turned if i == 1 else turned

    def gather_others(g):
        zero = jnp.zeros(full, jnp.float32)
        rows = jnp.concatenate([jnp.where(other_mask, x, zero) for x in g], axis=0)
        rows = rows[:, :ants] + rows[:, ants:]
        rows = jnp.concatenate(split3(rows), axis=0)
        size = 2 * times
        for k in range(2 * chunks):
            source = ((k + chunks) % (2 * chunks)) * width
            got = jnp.dot(
                rows, hot[:, source : source + width], preferred_element_type=jnp.float32
            )
            got = got[0:size] + got[size : 2 * size] + got[2 * size : 3 * size]
            g_ref[0, :, k * width : (k + 1) * width] = got[:times]
            g_ref[1, :, k * width : (k + 1) * width] = got[times:]

    def normal(g):
        for k in range(2 * chunks):
            here = slice(k * width, (k + 1) * width)
            m = (c_ref[0, :, here], c_ref[1, :, here])
            y = (g_ref[0, :, here], g_ref[1, :, here])
            x = cmul(m, y)
            parts = [[], [], []]
            for tile in (x[0], x[1], c_ref[2, :, here] * power(y)):
                high = tile.astype(jnp.bfloat16).astype(jnp.float32)
                rest = tile - high
                middle = rest.astype(jnp.bfloat16).astype(jnp.float32)
                for part, value in zip(parts, (high, middle, rest - middle)):
                    part.append(value)
            filler = [jnp.zeros((times, width), jnp.float32)]
            stacked = jnp.concatenate(parts[0] + parts[1] + parts[2] + filler, axis=0)
            terms[:, here] = stacked.astype(jnp.bfloat16)
        got = lax.dot_general(
            terms[...],
            hot[...],
            (((1,), (1,)), ((), ())),
            preferred_element_type=jnp.float32,
        )
        size = 3 * times
        got = got[0:size] + got[size : 2 * size] + got[2 * size : 3 * size]
        got = jnp.concatenate([got, got], axis=1)
        zero = jnp.zeros(full, jnp.float32)
        real, imag, e = [
            jnp.where(own_mask, got[i * times : (i + 1) * times], zero) for i in range(3)
        ]
        return (real - g[0] * e, imag - g[1] * e), e

    def over_times(x):
        return jnp.sum(x, axis=0, keepdims=True)

    owners = chunks
    all_own = owners == n_freq

    def owns(index):
        return True if all_own else index < owners

    for sweep in range(SWEEPS):
        g, band_delay, phasor = chain()
        rows = antenna_rows(g)
        for c in range(chunks):
            gp, gq = both(rows, c)
            r = residual_of(c, gp, gq)
            s_ref[sweep, c] = power(r[0][0]) + power(r[0][1]) + power(r[1][0]) + power(r[1][1])
        if sweep == 0:
            pl.semaphore_wait(barrier, n_freq * n_tm - 1)

        def scatter_copy(step):
            peer = lax.rem(f_me + step, n_freq)
            return remote(
                s_ref.at[sweep, peer],
                rs_ref.at[sweep, step],
                rs_sem.at[sweep],
                step,
                "freq",
                n_freq,
                f_me,
            )

        def send_part(step):
            peer = lax.rem(f_me + step, n_freq)
            maybe(owns(peer), lambda: scatter_copy(step).start())

        each_peer(n_freq, send_part)

        gather_others(g)

        def own_copy(step):
            return remote(
                w_ref.at[sweep, f_me],
                w_ref.at[sweep, f_me],
                ag_sem.at[sweep],
                step,
                "freq",
                n_freq,
                f_me,
            )

        def reduce_own():
            def arrive(step):
                pltpu.make_async_copy(
                    rs_ref.at[sweep, step], rs_ref.at[sweep, step], rs_sem.at[sweep, 1, step]
                ).wait()

            each_peer(n_freq, arrive)
            total = s_ref[sweep, f_me] + jnp.sum(rs_ref[sweep, 1:n_freq], axis=0)
            w_ref[sweep, f_me] = 1.0 / (total / (4 * channels) + EPSILON)
            each_peer(n_freq, lambda step: own_copy(step).start())

        maybe(owns(f_me), reduce_own)

        def receive_weights(step):
            origin = lax.rem(f_me + n_freq - step, n_freq)

            def arrive():
                pltpu.make_async_copy(
                    w_ref.at[sweep, 0], w_ref.at[sweep, 0], ag_sem.at[sweep, 1, step]
                ).wait()

            maybe(owns(origin), arrive)

        each_peer(n_freq, receive_weights)

        def sent(step):
            peer = lax.rem(f_me + step, n_freq)
            maybe(owns(peer), lambda: scatter_copy(step).wait_send())
            maybe(owns(f_me), lambda: own_copy(step).wait_send())

        each_peer(n_freq, sent)

        for c in range(chunks):
            put_matrices(c, w_ref[sweep, c])
        a, e = normal(g)
        n = conj_mul(band_delay, a)
        d = power(band_delay) * e
        rows_out = []
        for value in (n[0], n[1], d):
            for i in range(intervals):
                span = slice(i * INTERVAL_TIMES, (i + 1) * INTERVAL_TIMES)
                rows_out.append(over_times(value[span]))
        tile = stack_rows(rows_out, time_ref.shape[2])
        total = exchange(time_ref.at[sweep], tile, time_sem.at[sweep], "freq", n_freq, f_me)
        part = [total[i : i + 1] for i in range(3 * intervals)]
        g_time = tuple(
            g_time[p]
            + spread(
                [
                    DAMPING * part[p * intervals + i] / part[2 * intervals + i]
                    for i in range(intervals)
                ]
            )
            for p in range(2)
        )

        g, band_delay, phasor = chain()
        gather_others(g)
        a, e = normal(g)
        other = cmul(g_time, phasor)
        n = conj_mul(other, a)
        tile = stack_rows([over_times(x) for x in (n[0], n[1], power(other) * e)], 8)
        total = exchange(band_ref.at[sweep], tile, band_sem.at[sweep], "tm", n_tm, t_me)
        g_band = tuple(
            g_band[p] + jnp.broadcast_to(DAMPING * total[p : p + 1] / total[2:3], full)
            for p in range(2)
        )

        g, band_delay, phasor = chain()
        gather_others(g)
        a, e = normal(g)
        n = turning * conj_mul(g, a)[1]
        d = turning * turning * power(g) * e
        tile = stack_rows([over_times(n), over_times(d)], 2)
        total = exchange_all(turn_ref.at[sweep], tile, turn_sem.at[sweep])
        turns = turns + jnp.broadcast_to(DAMPING * total[0:1] / total[1:2], full)

    g, band_delay, phasor = chain()
    rows = antenna_rows(g)
    for c in range(chunks):
        gp, gq = both(rows, c)
        r = residual_of(c, gp, gq)
        stop = min(baselines, (c + 1) * width)
        here = slice(c * width, stop)
        size = stop - c * width
        for i in range(2):
            for a in range(2):
                for b in range(2):
                    out_residual[4 * i + 2 * a + b, :, here] = r[a][b][i][:, :size]
        out_weights[:, here] = w_ref[SWEEPS - 1, c][:, :size]
    rows_out = [
        g_time[p][i * INTERVAL_TIMES : i * INTERVAL_TIMES + 1]
        for p in range(2)
        for i in range(intervals)
    ]
    rows_out += [g_band[0][0:1], g_band[1][0:1], turns[0:1]]
    out_params[...] = stack_rows(rows_out, out_params.shape[0])


def write_kernel(intervals, params, weights, residual, o_time, o_band, o_delay, o_weights, o_residual):
    ants = LANES // POLS
    for p in range(POLS):
        half = slice(p * ants, (p + 1) * ants)
        for part in range(2):
            o_time[part, p] = params[part * intervals : (part + 1) * intervals, half]
            o_band[part, p] = params[2 * intervals + part : 2 * intervals + part + 1, half]
        o_delay[p : p + 1, :] = params[2 * intervals + 2 : 2 * intervals + 3, half]
    o_weights[...] = weights[...]
    for i in range(8):
        o_residual[i // 4, i % 4, :, 0, :] = residual[i]


def ceil_to(value, step):
    return -(-value // step) * step


def shards(n_freq, n_tm, vis, sky, gain_time, gain_band, delay_start, first, second):
    times, local_channels, baselines = vis.shape[2:]
    antennas = gain_time.shape[-1]
    assert local_channels == 1 and POLS * antennas == LANES
    intervals = times // INTERVAL_TIMES
    assert times == 8 and INTERVAL_TIMES == POLS * POLS
    channels = local_channels * n_freq
    tiles = -(-baselines // LANES)
    chunks = max(c for c in range(1, min(n_freq, tiles) + 1) if tiles % c == 0)
    width = tiles * LANES // chunks
    padded = tiles * LANES
    flat = (8, times, baselines)
    count = 2 * intervals + 3
    height = ceil_to(count, 8)
    sizes = (n_freq, n_tm, channels, times, baselines, chunks, width)
    f32 = jnp.float32
    vmem = pl.BlockSpec(memory_space=pltpu.VMEM)
    sems = [
        pltpu.SemaphoreType.DMA((SWEEPS, 2) + counts)
        for counts in ((n_freq,), (n_freq,), (n_freq,), (n_tm,), (n_tm, n_freq))
    ]
    solved, weights, residual = pl.pallas_call(
        functools.partial(kernel, sizes),
        out_shape=(
            jax.ShapeDtypeStruct((height, LANES), f32),
            jax.ShapeDtypeStruct((times, baselines), f32),
            jax.ShapeDtypeStruct(flat, f32),
        ),
        in_specs=[pl.BlockSpec(memory_space=pl.ANY)] * 2 + [vmem] * 5,
        out_specs=(vmem,) * 3,
        scratch_shapes=[
            pltpu.VMEM(vis.shape, f32),
            pltpu.VMEM(sky.shape, f32),
            pltpu.SemaphoreType.DMA((2,)),
            pltpu.VMEM((8, times, padded), f32),
            pltpu.VMEM((8, times, padded), f32),
            pltpu.VMEM((antennas, 2 * padded), jnp.bfloat16),
            pltpu.VMEM((8, times, padded), f32),
            pltpu.VMEM((4, times, padded), f32),
            pltpu.VMEM((3, times, 2 * padded), f32),
            pltpu.VMEM((2, times, 2 * padded), f32),
            pltpu.VMEM((10 * times, 2 * padded), jnp.bfloat16),
            pltpu.VMEM((SWEEPS, chunks, times, width), f32),
            pltpu.VMEM((SWEEPS, n_freq, times, width), f32),
            pltpu.VMEM((SWEEPS, chunks, times, width), f32),
            pltpu.VMEM((SWEEPS, n_freq, ceil_to(3 * intervals, 8), LANES), f32),
            pltpu.VMEM((SWEEPS, n_tm, 8, LANES), f32),
            pltpu.VMEM((SWEEPS, n_tm, n_freq, 2, LANES), f32),
            *sems,
        ],
        compiler_params=pltpu.CompilerParams(collective_id=0, has_side_effects=True),
    )(
        vis,
        sky,
        gain_time,
        gain_band,
        delay_start,
        first.reshape(1, baselines),
        second.reshape(1, baselines),
    )
    return pl.pallas_call(
        functools.partial(write_kernel, intervals),
        out_shape=tuple(
            jax.ShapeDtypeStruct(like.shape, f32)
            for like in (gain_time, gain_band, delay_start, weights, vis)
        ),
        in_specs=[vmem] * 3,
        out_specs=(vmem,) * 5,
    )(solved, weights, residual)


def solution(mesh):
    in_specs = (
        P(None, None, "tm", "freq", None),
        P(None, None, "tm", "freq", None),
        P(None, None, "tm", None),
        P(None, None, "freq", None),
        P(),
        P(),
        P(),
    )
    out_specs = (
        P(None, None, "tm", None),
        P(None, None, "freq", None),
        P(),
        P("tm", None),
        P(None, None, "tm", "freq", None),
    )
    body = functools.partial(shards, mesh.shape["freq"], mesh.shape["tm"])
    return jax.shard_map(body, mesh=mesh, in_specs=in_specs, out_specs=out_specs, check_vma=False)
```
